32 devices in a mesh: grp: 4 (over z), shard: 8 (over y, x, core).
Axes of the slice: x: 2, y: 2, z: 4, core: 2. Of those that a mesh axis runs over, the one named last changes fastest.
Arguments:
- table: float32 [1024, 8, 128], P('shard')
- table_first: float32 [1024, 8, 128], P('shard'), may hold values from -3 to 3
- table_second: float32 [1024, 8, 128], P('shard')
- slot_table: int32 [1024], P('shard'), may hold values from 0 to 25
- touched: int32 [4, 256], P('grp', 'shard'), may hold values from 0 to 1023, as said below
- emb_grads: bfloat16 [4, 256, 8, 128], P('grp', 'shard'), may hold values from -6 to 6
- block_slot: int32 [1024], replicated, may hold values from 0 to 1023, as said below
- dense_x: bfloat16 [13, 131072], P(None, ('grp', 'shard')), may hold values from -6 to 6
- dense_cot: bfloat16 [131072, 128], P(('grp', 'shard')), may hold values from -0.15625 to 0.15625
- w_one: float32 [13, 512], replicated, may hold values from -1.75 to 1.75
- w_two: float32 [512, 256], replicated, may hold values from -0.25 to 0.25
- w_three: float32 [256, 128], replicated, may hold values from -0.375 to 0.375
- first_one: float32 [13, 512], replicated, may hold values from -3 to 3
- first_two: float32 [512, 256], replicated, may hold values from -3 to 3
- first_three: float32 [256, 128], replicated, may hold values from -3 to 3
- second_one: float32 [13, 512], replicated, may hold values from 0.001 to 0.3
- second_two: float32 [512, 256], replicated, may hold values from 0.001 to 0.3
- second_three: float32 [256, 128], replicated, may hold values from 0.001 to 0.3
Outputs:
- new_table: float32 [1024, 8, 128], P('shard')
- new_table_first: float32 [1024, 8, 128], P('shard')
- new_table_second: float32 [1024, 8, 128], P('shard')
- new_w_one: float32 [13, 512], replicated
- new_w_two: float32 [512, 256], replicated
- new_w_three: float32 [256, 128], replicated
- new_first_one: float32 [13, 512], replicated
- new_first_two: float32 [512, 256], replicated
- new_first_three: float32 [256, 128], replicated
- new_second_one: float32 [13, 512], replicated
- new_second_two: float32 [512, 256], replicated
- new_second_three: float32 [256, 128], replicated
The draws below stay inside these ranges and needn't reach their ends.
Inputs may be any that keep to these rules, and one draw needn't show every extreme that they name: `touched`: each device's 32 ids are distinct; at most 8 of them have block_slot // 128 equal to any one shard, and in every draw some shard gets exactly 8 from every device. `block_slot`: A permutation of the 1024 slots.
All inputs are finite; a program needn't handle non-finite values.
Results may differ from the reference program's by a relative error of at most 0.0037.
Values may be sent and summed in bfloat16 or wider, within the bound.
A program may use at most 128 MiB of HBM per device.

```python
import math
import jax
import jax.numpy as jnp
from jax import lax

E = 128
DIN = 13
H1 = 512
H2 = 256
TABLES = 26
BLK = 8
CAP = 8
NB_DEV = 128
TOK_DEV = 4096
K = 32
NB = 1024
TOKENS = 131072
N_GRP = 4
N_SHARD = 8


def common_slots(key):
    forward = jax.random.permutation(jax.random.fold_in(key, 11), NB).astype(jnp.int32)
    inverse = jnp.zeros((NB,), jnp.int32).at[forward].set(jnp.arange(NB, dtype=jnp.int32))
    return (forward, inverse)


def draw_block_slot(key, part):
    return common_slots(key)[0]


def draw_touched(key, part):
    forward, inverse = common_slots(key)
    devices_all = N_GRP * N_SHARD
    candidates = N_SHARD * CAP
    live_count = max(CAP, NB_DEV * 5 // 8)
    hottest = jax.random.randint(jax.random.fold_in(key, 12), (), 0, N_SHARD)
    owner_bias = jax.random.randint(jax.random.fold_in(key, 13), (devices_all, N_SHARD), 0, 4)
    owner_bias = jnp.where(jnp.arange(N_SHARD)[None, :] == hottest, 8, owner_bias)
    noise_keys = jax.random.split(jax.random.fold_in(key, 14), devices_all)
    noise = jax.vmap(lambda subkey: jax.random.permutation(subkey, candidates))(noise_keys).astype(jnp.int32)
    cand_owner = jnp.arange(candidates, dtype=jnp.int32) // CAP
    scores = owner_bias[:, cand_owner] * 1048576 + noise
    unused, chosen = lax.top_k(scores, K)
    owner_keys = jax.random.split(jax.random.fold_in(key, 17), N_SHARD)
    live_sets = jax.vmap(lambda subkey: jax.random.permutation(subkey, NB_DEV)[:live_count])(owner_keys).astype(jnp.int32)
    row_keys = jax.random.split(jax.random.fold_in(key, 15), devices_all * N_SHARD)
    live_pick = jax.vmap(lambda subkey: jax.random.permutation(subkey, live_count)[:CAP])(row_keys).astype(jnp.int32)
    live_pick = live_pick.reshape(devices_all, N_SHARD, CAP)
    owner_rows = jnp.arange(N_SHARD, dtype=jnp.int32)[None, :, None]
    local_rows = live_sets[owner_rows, live_pick].reshape(devices_all, candidates)
    local_pick = jnp.take_along_axis(local_rows, chosen, axis=1)
    slot_pick = chosen // CAP * NB_DEV + local_pick
    block_ids = inverse[slot_pick]
    order_keys = jax.random.split(jax.random.fold_in(key, 16), devices_all)
    orders = jax.vmap(lambda subkey: jax.random.permutation(subkey, K))(order_keys).astype(jnp.int32)
    block_ids = jnp.take_along_axis(block_ids, orders, axis=1)
    return block_ids.reshape(N_GRP, N_SHARD * K).astype(jnp.int32)


def slot_rise():
    slot_pos = jnp.arange(NB, dtype=jnp.float32)
    return 1.0 + 2.0 * slot_pos / max(NB - 1, 1)


def draw_table(key, part):
    rise = slot_rise()
    row_scale = 10.0 ** jax.random.uniform(jax.random.fold_in(key, 21), (NB, BLK, 1), jnp.float32)
    col_scale = 10.0 ** (jax.random.uniform(jax.random.fold_in(key, 22), (1, 1, E), jnp.float32) - 1.0)
    base = jax.random.normal(jax.random.fold_in(key, 23), (NB, BLK, E), jnp.float32)
    return (base * row_scale * col_scale * rise[:, None, None]).astype(jnp.float32)


def draw_table_second(key, part):
    rise = slot_rise()
    expo = jax.random.uniform(jax.random.fold_in(key, 31), (NB, BLK, E), jnp.float32, -3.0, -0.5)
    return (10.0 ** expo / (rise * rise)[:, None, None]).astype(jnp.float32)


def place_ends(drawn, rng, smallest, largest):
    dims = drawn.shape
    place = [jax.random.randint(jax.random.fold_in(rng, axis), (), 0, dims[axis]) for axis in range(len(dims))]
    drawn = drawn.at[tuple(place)].set(smallest)
    longest = dims.index(max(dims))
    place[longest] = (place[longest] + 1) % dims[longest]
    return drawn.at[tuple(place)].set(largest)


def levels(key, shape, cuts, low, top_value):
    loudness = 1.0
    for position, blocks in cuts:
        heights = jax.random.uniform(jax.random.fold_in(jax.random.fold_in(key, 6), position), (blocks,), jnp.float32, low / len(cuts), top_value / len(cuts))
        loudness = loudness * jnp.repeat(jnp.exp(heights), shape[position] // blocks).reshape((-1,) + (1,) * (len(shape) - 1 - position))
    return loudness


def gaussian(own_key, extent, width, most, cuts=(), kind=jnp.bfloat16):
    gain = levels(own_key, extent, cuts, -0.22, 0.18) if cuts else 1.0
    entries = jax.random.normal(own_key, extent, jnp.float32) * width * gain
    return jnp.minimum(jnp.maximum(entries, -most), most).astype(kind)


def setup_inputs(seed: int = 0) -> dict:
    keys = jax.random.split(jax.random.key(seed), 19)
    return {
        "table": draw_table(jax.random.fold_in(keys[18], 71), 0),
        "table_first": gaussian(keys[1], (NB, BLK, E), 0.2, 3.0, ((0, 8),), jnp.float32),
        "table_second": draw_table_second(jax.random.fold_in(keys[18], 71), 0),
        "slot_table": place_ends(jax.random.randint(keys[3], (NB,), 0, TABLES), jax.random.fold_in(keys[3], 1), 0, TABLES - 1).astype(jnp.int32),
        "touched": draw_touched(jax.random.fold_in(keys[18], 71), 0),
        "emb_grads": gaussian(keys[5], (N_GRP, N_SHARD * K, BLK, E), 1.0, 6.0, ((0, 4), (1, 8))),
        "block_slot": draw_block_slot(jax.random.fold_in(keys[18], 71), 0),
        "dense_x": gaussian(keys[7], (DIN, TOKENS), 1.0, 6.0, ((1, 32),)),
        "dense_cot": gaussian(keys[8], (TOKENS, E), (4 * TOKENS ** -0.5), 0.15625, ((0, 32),)),
        "w_one": gaussian(keys[9], (DIN, H1), DIN ** -0.5, 1.75, (), jnp.float32),
        "w_two": gaussian(keys[10], (H1, H2), H1 ** -0.5, 0.25, (), jnp.float32),
        "w_three": gaussian(keys[11], (H2, E), H2 ** -0.5, 0.375, (), jnp.float32),
        "first_one": gaussian(keys[12], (DIN, H1), 0.2, 3.0, (), jnp.float32),
        "first_two": gaussian(keys[13], (H1, H2), 0.2, 3.0, (), jnp.float32),
        "first_three": gaussian(keys[14], (H2, E), 0.2, 3.0, (), jnp.float32),
        "second_one": jnp.clip(jnp.exp(jax.random.uniform(keys[15], (DIN, H1), jnp.float32, math.log(0.001), math.log(0.3))), 0.001, 0.3),
        "second_two": jnp.clip(jnp.exp(jax.random.uniform(keys[16], (H1, H2), jnp.float32, math.log(0.001), math.log(0.3))), 0.001, 0.3),
        "second_three": jnp.clip(jnp.exp(jax.random.uniform(keys[17], (H2, E), jnp.float32, math.log(0.001), math.log(0.3))), 0.001, 0.3),
    }


beta_one = 0.9
beta_two = 0.999
corr_first = 1.0 - 0.9 ** 10
corr_second = 1.0 - 0.999 ** 10
adam_eps = 1e-06
decay_rate = 0.01
learn_rate = 0.1
ratio_eps = 1e-06

def silu_slope(pre_value):
    logistic = jax.nn.sigmoid(pre_value)
    return logistic * (1.0 + pre_value * (1.0 - logistic))

def tower_grads(dense_x, dense_cot, w_one, w_two, w_three):
    w_one_bf = w_one.astype(jnp.bfloat16)
    w_two_bf = w_two.astype(jnp.bfloat16)
    w_three_bf = w_three.astype(jnp.bfloat16)
    pre_one = lax.dot_general(dense_x, w_one_bf, (((0,), (0,)), ((), ())), preferred_element_type=jnp.float32)
    hidden_one = jax.nn.silu(pre_one).astype(jnp.bfloat16)
    pre_two = jnp.dot(hidden_one, w_two_bf, preferred_element_type=jnp.float32)
    hidden_two = jax.nn.silu(pre_two).astype(jnp.bfloat16)
    grad_three = lax.dot_general(hidden_two, dense_cot, (((0,), (0,)), ((), ())), preferred_element_type=jnp.float32)
    back_two = (lax.dot_general(dense_cot, w_three_bf, (((1,), (1,)), ((), ())), preferred_element_type=jnp.float32) * silu_slope(pre_two)).astype(jnp.bfloat16)
    grad_two = lax.dot_general(hidden_one, back_two, (((0,), (0,)), ((), ())), preferred_element_type=jnp.float32)
    back_one = (lax.dot_general(back_two, w_two_bf, (((1,), (1,)), ((), ())), preferred_element_type=jnp.float32) * silu_slope(pre_one)).astype(jnp.bfloat16)
    grad_one = jnp.dot(dense_x, back_one, preferred_element_type=jnp.float32)
    return (grad_one, grad_two, grad_three)

def lamb_dense(weight, first_in, second_in, gradient):
    first_out = beta_one * first_in + (1.0 - beta_one) * gradient
    second_out = beta_two * second_in + (1.0 - beta_two) * gradient * gradient
    update = first_out / corr_first / (jnp.sqrt(second_out / corr_second) + adam_eps) + decay_rate * weight
    trust_ratio = jnp.sqrt(jnp.sum(weight * weight)) / (jnp.sqrt(jnp.sum(update * update)) + ratio_eps)
    return (weight - learn_rate * trust_ratio * update, first_out, second_out)

def reference(table, table_first, table_second, slot_table, touched, emb_grads, block_slot, dense_x, dense_cot, w_one, w_two, w_three, first_one, first_two, first_three, second_one, second_two, second_three):
    slot_index = block_slot[touched].reshape(-1)
    flat_grads = emb_grads.reshape(-1, BLK, E).astype(jnp.float32)
    emb_grad = jnp.zeros((NB, BLK, E), jnp.float32).at[slot_index].add(flat_grads)
    hits = jnp.zeros((NB,), jnp.float32).at[slot_index].add(jnp.ones(slot_index.shape, jnp.float32))
    touched_mask = (hits > 0.5)[:, None, None]
    new_first = jnp.where(touched_mask, beta_one * table_first + (1.0 - beta_one) * emb_grad, table_first)
    new_second = jnp.where(touched_mask, beta_two * table_second + (1.0 - beta_two) * emb_grad * emb_grad, table_second)
    update = jnp.where(touched_mask, new_first / corr_first / (jnp.sqrt(new_second / corr_second) + adam_eps) + decay_rate * table, 0.0)
    weight_sq = jax.ops.segment_sum(lax.optimization_barrier(jnp.sum(table * table, axis=(1, 2))), slot_table, TABLES)
    update_sq = jax.ops.segment_sum(lax.optimization_barrier(jnp.sum(update * update, axis=(1, 2))), slot_table, TABLES)
    table_ratio = jnp.sqrt(weight_sq) / (jnp.sqrt(update_sq) + ratio_eps)
    new_table = table - learn_rate * table_ratio[slot_table][:, None, None] * update
    blocks_all = N_GRP * N_SHARD
    x_blocks = dense_x.reshape(DIN, blocks_all, TOK_DEV).transpose(1, 0, 2)
    cot_blocks = dense_cot.reshape(blocks_all, TOK_DEV, E)

    def accumulate(totals, inputs):
        terms = tower_grads(inputs[0], inputs[1], w_one, w_two, w_three)
        return ((totals[0] + terms[0], totals[1] + terms[1], totals[2] + terms[2]), None)
    start_sums = (jnp.zeros((DIN, H1), jnp.float32), jnp.zeros((H1, H2), jnp.float32), jnp.zeros((H2, E), jnp.float32))
    grads, unused = lax.scan(accumulate, start_sums, (x_blocks, cot_blocks))
    layer_one = lamb_dense(w_one, first_one, second_one, grads[0])
    layer_two = lamb_dense(w_two, first_two, second_two, grads[1])
    layer_three = lamb_dense(w_three, first_three, second_three, grads[2])
    return (new_table, new_first, new_second, layer_one[0], layer_two[0], layer_three[0], layer_one[1], layer_two[1], layer_three[1], layer_one[2], layer_two[2], layer_three[2])
```

```python
import functools
import jax
import jax.numpy as jnp
from jax import lax
from jax.experimental import pallas as pl
from jax.experimental.pallas import tpu as pltpu
from jax.sharding import PartitionSpec as P

TABLES = 26
CAP = 8

beta_one = 0.9
beta_two = 0.999
corr_first = 1.0 - 0.9**10
corr_second = 1.0 - 0.999**10
adam_eps = 1e-06
decay_rate = 0.01
learn_rate = 0.1
ratio_eps = 1e-06

MESH = pl.DeviceIdType.MESH
F32 = jnp.float32
BF16 = jnp.bfloat16
NN = (((1,), (0,)), ((), ()))
NT = (((1,), (1,)), ((), ()))
TN = (((0,), (0,)), ((), ()))


def mm(a, b, dims=NN):
    return lax.dot_general(a, b, dims, preferred_element_type=F32)


def iota(shape, axis):
    return lax.broadcasted_iota(jnp.int32, shape, axis).astype(F32)


def to_col(row, eye):
    return jnp.sum(jnp.where(eye, row, 0.0), axis=1, keepdims=True)


def to_row(col, eye):
    return jnp.sum(jnp.where(eye, col, 0.0), axis=0, keepdims=True)


def square_eye(count):
    return iota((count, count), 0) == iota((count, count), 1)


def gate(pre):
    logistic = 0.5 * jnp.tanh(0.5 * pre) + 0.5
    hidden = pre * logistic
    return hidden, logistic + hidden * (1.0 - logistic)


def adam(first_in, second_in, gradient, weight):
    first_out = beta_one * first_in + (1.0 - beta_one) * gradient
    second_out = beta_two * second_in + (1.0 - beta_two) * gradient * gradient
    update = (
        first_out / corr_first / (jnp.sqrt(second_out / corr_second) + adam_eps)
        + decay_rate * weight
    )
    return first_out, second_out, update


def exchange_kernel(
    grps,
    shards,
    chunk,
    touched,
    block_slot,
    slot_table,
    emb_grads,
    x,
    cot,
    w_one,
    w_two,
    w_three,
    table,
    table_first,
    table_second,
    emb_out,
    rate_out,
    g_one,
    g_two,
    g_three,
    w1t,
    w2t,
    w2b,
    w3b,
    slope_buf,
    back_buf,
    acc_one,
    acc_two,
    acc_three,
    rows_f32,
    e_send,
    e_recv,
    p2_send,
    p2_recv,
    p3_send,
    p3_recv,
    z2,
    z3,
    a2,
    a3,
    s1,
    y1,
    stats,
    plane_ssem,
    plane_rsem,
    z_ssem,
    z_rsem,
):
    g = lax.axis_index("grp")
    s = lax.axis_index("shard")
    width = emb_grads.shape[1]
    block_rows = 8
    count = touched.shape[1]
    slots = block_slot.shape[1]
    local_blocks = slot_table.shape[1]
    tokens = x.shape[1]
    din = x.shape[0]

    barrier = pltpu.get_barrier_semaphore()
    for k in range(1, shards):
        pl.semaphore_signal(barrier, inc=1, device_id=(g, lax.rem(s + k, shards)), device_id_type=MESH)
    for k in range(1, grps):
        pl.semaphore_signal(barrier, inc=1, device_id=(lax.rem(g + k, grps), s), device_id_type=MESH)

    def plane(phase, k, src, dst):
        return pltpu.make_async_remote_copy(
            src_ref=src,
            dst_ref=dst,
            send_sem=plane_ssem.at[phase, k],
            recv_sem=plane_rsem.at[phase, k],
            device_id=(g, lax.rem(s + k, shards)),
            device_id_type=MESH,
        )

    def along(phase, k, src, dst):
        return pltpu.make_async_remote_copy(
            src_ref=src,
            dst_ref=dst,
            send_sem=z_ssem.at[phase, k],
            recv_sem=z_rsem.at[phase, k],
            device_id=(lax.rem(g + k, grps), s),
            device_id_type=MESH,
        )

    def plane_scatter(phase, src, dst):
        out = [plane(phase, k, src.at[lax.rem(s + k, shards)], dst.at[s]) for k in range(1, shards)]
        for c in out:
            c.start()
        return out

    def plane_spread(phase, buf):
        out = [plane(phase, k, buf.at[s], buf.at[s]) for k in range(1, shards)]
        for c in out:
            c.start()
        return out

    def z_spread(phase, buf):
        out = [along(phase, k, buf.at[g], buf.at[g]) for k in range(1, grps)]
        for c in out:
            c.start()
        return out

    def recv(copies):
        for c in copies:
            c.wait_recv()

    eye = square_eye(count)
    touched_col = to_col(touched[...].astype(F32), eye)
    hot = touched_col == iota((count, slots), 1)
    slot_col = jnp.sum(jnp.where(hot, block_slot[...].astype(F32), 0.0), axis=1, keepdims=True)
    slot_row = to_row(slot_col, eye)
    owner_col = jnp.floor((slot_col + 0.5) / local_blocks)
    owner_row = jnp.floor((slot_row + 0.5) / local_blocks)
    local_row = slot_row - owner_row * local_blocks
    earlier = (owner_col == owner_row) & (iota((count, count), 0) < iota((count, count), 1))
    rank_row = jnp.sum(jnp.where(earlier, 1.0, 0.0), axis=0, keepdims=True)
    send_row = owner_row * CAP + rank_row
    picker = iota((shards * CAP, count), 0) == send_row
    pick_f32 = jnp.where(picker, 1.0, 0.0)
    pick_bf = pick_f32.astype(BF16)
    filled = jnp.sum(pick_f32, axis=1, keepdims=True)
    local_col = jnp.sum(jnp.where(picker, local_row, 0.0), axis=1, keepdims=True)
    local_col = jnp.where(filled > 0.5, local_col, -1.0)
    rows_f32[...] = emb_grads[...].astype(F32)
    for r in range(block_rows):
        part = rows_f32[pl.ds(r, count, stride=block_rows), :].astype(BF16)
        picked = mm(pick_bf, part).reshape(shards, CAP, width)
        e_send[:, :, r * width : (r + 1) * width] = picked.astype(BF16)
    lanes = jnp.broadcast_to(local_col, (shards * CAP, width)).reshape(shards, CAP, width)
    e_send[:, :, block_rows * width :] = lanes.astype(BF16)
    e_recv[g, s] = e_send[s]

    pl.semaphore_wait(barrier, shards + grps - 2)
    sends = []
    e_plane = [
        plane(0, k, e_send.at[lax.rem(s + k, shards)], e_recv.at[g, s]) for k in range(1, shards)
    ]
    for c in e_plane:
        c.start()
    sends += e_plane

    w1t[...] = w_one[...].T.astype(BF16)
    w2t[...] = w_two[...].T.astype(BF16)
    w2b[...] = w_two[...].astype(BF16)
    w3b[...] = w_three[...].astype(BF16)
    acc_one[...] = jnp.zeros_like(acc_one)
    acc_two[...] = jnp.zeros_like(acc_two)
    acc_three[...] = jnp.zeros_like(acc_three)

    def forward(i, carry):
        tok = pl.ds(pl.multiple_of(i * chunk, chunk), chunk)
        hid, slope = gate(mm(w1t[...], x[:, tok]))
        hidden_one = hid.astype(BF16)
        slope_buf[:, tok] = slope
        hid, slope = gate(mm(w2t[...], hidden_one))
        c = cot[tok, :]
        acc_three[...] += mm(hid.astype(BF16), c)
        back = (mm(w3b[...], c, NT) * slope).astype(BF16)
        back_buf[:, tok] = back
        acc_two[...] += mm(hidden_one, back, NT)
        return carry

    def backward(i, carry):
        tok = pl.ds(pl.multiple_of(i * chunk, chunk), chunk)
        back = (mm(w2b[...], back_buf[:, tok]) * slope_buf[:, tok]).astype(BF16)
        acc_one[0:din, :] += mm(x[:, tok], back, NT)
        return carry

    steps = tokens // chunk
    head = steps // 2
    lax.fori_loop(0, head, forward, 0)
    recv(e_plane)
    e_z = z_spread(0, e_recv)
    sends += e_z
    lax.fori_loop(head, steps, forward, 0)

    p2_send[...] = acc_two[...].reshape(p2_send.shape).astype(BF16)
    p3_send[...] = acc_three[...].reshape(p3_send.shape).astype(BF16)
    p2_recv[s] = p2_send[s]
    p3_recv[s] = p3_send[s]
    c_p2 = plane_scatter(1, p2_send, p2_recv)
    c_p3 = plane_scatter(2, p3_send, p3_recv)
    sends += c_p2 + c_p3

    lax.fori_loop(0, steps, backward, 0)
    s1[s] = acc_one[...].astype(BF16)
    c_s1 = plane_spread(3, s1)
    sends += c_s1

    def total(buf, n):
        out = buf[0].astype(F32)
        for i in range(1, n):
            out += buf[i].astype(F32)
        return out

    recv(c_p2)
    z2[g] = total(p2_recv, shards).astype(BF16)
    c_z2 = z_spread(1, z2)
    recv(c_p3)
    z3[g] = total(p3_recv, shards).astype(BF16)
    c_z3 = z_spread(2, z3)
    recv(c_s1)
    y1[g] = total(s1, shards).astype(BF16)
    c_y1 = z_spread(3, y1)
    sends += c_z2 + c_z3 + c_y1

    recv(e_z)
    pieces = grps * shards * CAP
    row_width = block_rows * width
    tags = e_recv[:, :, :, row_width:].astype(F32).reshape(pieces, width)
    match = jnp.where(tags[:, 0:1] == iota((pieces, local_blocks), 1), 1.0, 0.0)
    match_t = match.T.astype(BF16)
    hits = mm(match_t, jnp.ones((pieces, width), BF16)) > 0.5
    row_weight = jnp.zeros((local_blocks, width), F32)
    row_update = jnp.zeros((local_blocks, width), F32)
    for r in range(block_rows):
        at = pl.ds(r, local_blocks, stride=block_rows)
        rows = e_recv[:, :, :, r * width : (r + 1) * width].astype(F32)
        summed = mm(match_t, rows.reshape(pieces, width).astype(BF16))
        emb_out[at, :] = summed
        weight = table[at, :]
        update = adam(table_first[at, :], table_second[at, :], summed, weight)[2]
        update = jnp.where(hits, update, 0.0)
        row_weight += weight * weight
        row_update += update * update
    slot_eye = square_eye(local_blocks)
    table_col = to_col(slot_table[...].astype(F32), slot_eye)
    table_hot = table_col == iota((local_blocks, 128), 1)
    weight_col = jnp.sum(row_weight, axis=1, keepdims=True)
    update_col = jnp.sum(row_update, axis=1, keepdims=True)
    stats[s] = jnp.concatenate(
        [
            jnp.sum(jnp.where(table_hot, weight_col, 0.0), axis=0, keepdims=True),
            jnp.sum(jnp.where(table_hot, update_col, 0.0), axis=0, keepdims=True),
            jnp.zeros((6, 128), F32),
        ],
        axis=0,
    )
    c_st = plane_spread(4, stats)
    sends += c_st

    recv(c_z2)
    a2[s] = total(z2, grps).astype(BF16)
    c_a2 = plane_spread(5, a2)
    recv(c_z3)
    a3[s] = total(z3, grps).astype(BF16)
    c_a3 = plane_spread(6, a3)
    sends += c_a2 + c_a3
    recv(c_st)
    tot = total(stats, shards)
    ratio = jnp.sqrt(tot[0:1]) / (jnp.sqrt(tot[1:2]) + ratio_eps)
    ratio_col = jnp.sum(jnp.where(table_hot, ratio, 0.0), axis=1, keepdims=True)
    rate = jnp.where(hits, learn_rate * ratio_col, -1.0)
    for r in range(block_rows):
        rate_out[pl.ds(r, local_blocks, stride=block_rows), :] = rate
    recv(c_y1)
    g_one[...] = total(y1, grps)
    recv(c_a2)
    g_two[...] = a2[...].astype(F32).reshape(g_two.shape)
    recv(c_a3)
    g_three[...] = a3[...].astype(F32).reshape(g_three.shape)
    for c in sends:
        c.wait_send()


def lamb_kernel(
    emb, rate, table, tf, ts, g1, g2, g3, w1, w2, w3, f1, f2, f3, q1, q2, q3,
    o_t, o_tf, o_ts, o_w1, o_w2, o_w3, o_f1, o_f2, o_f3, o_q1, o_q2, o_q3,
):
    mask = rate[...] >= 0.0
    first, second, update = adam(tf[...], ts[...], emb[...], table[...])
    o_tf[...] = jnp.where(mask, first, tf[...])
    o_ts[...] = jnp.where(mask, second, ts[...])
    o_t[...] = jnp.where(mask, table[...] - rate[...] * update, table[...])
    for grad, w, f, q, ow, of, oq in (
        (g1, w1, f1, q1, o_w1, o_f1, o_q1),
        (g2, w2, f2, q2, o_w2, o_f2, o_q2),
        (g3, w3, f3, q3, o_w3, o_f3, o_q3),
    ):
        weight = w[...]
        first, second, update = adam(f[...], q[...], grad[0 : w.shape[0], :], weight)
        of[...] = first
        oq[...] = second
        trust = jnp.sqrt(jnp.sum(weight * weight, keepdims=True)) / (
            jnp.sqrt(jnp.sum(update * update, keepdims=True)) + ratio_eps
        )
        ow[...] = weight - learn_rate * trust * update


def body(
    table, table_first, table_second, slot_table, touched, emb_grads, block_slot,
    dense_x, dense_cot, w_one, w_two, w_three, first_one, first_two, first_three,
    second_one, second_two, second_three,
):
    shards = lax.axis_size("shard")
    grps = lax.axis_size("grp")
    blocks, block_rows, width = table.shape
    count = touched.shape[1]
    din, tokens = dense_x.shape
    h_one, h_two = w_two.shape
    out_dim = w_three.shape[1]
    chunk = min(512, tokens)
    din_pad = -(-din // 16) * 16
    flat = (blocks * block_rows, width)
    e_width = block_rows * width + width
    r2 = h_one // shards
    r3 = h_two // shards
    vmem = pl.BlockSpec(memory_space=pltpu.VMEM)
    t2, tf2, ts2 = (a.reshape(flat) for a in (table, table_first, table_second))
    sds = jax.ShapeDtypeStruct
    emb, rate, g1, g2, g3 = pl.pallas_call(
        functools.partial(exchange_kernel, grps, shards, chunk),
        out_shape=(
            sds(flat, F32),
            sds(flat, F32),
            sds((din_pad, h_one), F32),
            sds((h_one, h_two), F32),
            sds((h_two, out_dim), F32),
        ),
        in_specs=[vmem] * 12,
        out_specs=(vmem,) * 5,
        scratch_shapes=[
            pltpu.VMEM((h_one, din), BF16),
            pltpu.VMEM((h_two, h_one), BF16),
            pltpu.VMEM((h_one, h_two), BF16),
            pltpu.VMEM((h_two, out_dim), BF16),
            pltpu.VMEM((h_one, tokens), F32),
            pltpu.VMEM((h_two, tokens), BF16),
            pltpu.VMEM((din_pad, h_one), F32),
            pltpu.VMEM((h_one, h_two), F32),
            pltpu.VMEM((h_two, out_dim), F32),
            pltpu.VMEM((count * block_rows, width), F32),
            pltpu.VMEM((shards, CAP, e_width), BF16),
            pltpu.VMEM((grps, shards, CAP, e_width), BF16),
            pltpu.VMEM((shards, r2, h_two), BF16),
            pltpu.VMEM((shards, r2, h_two), BF16),
            pltpu.VMEM((shards, r3, out_dim), BF16),
            pltpu.VMEM((shards, r3, out_dim), BF16),
            pltpu.VMEM((grps, r2, h_two), BF16),
            pltpu.VMEM((grps, r3, out_dim), BF16),
            pltpu.VMEM((shards, r2, h_two), BF16),
            pltpu.VMEM((shards, r3, out_dim), BF16),
            pltpu.VMEM((shards, din_pad, h_one), BF16),
            pltpu.VMEM((grps, din_pad, h_one), BF16),
            pltpu.VMEM((shards, 8, 128), F32),
            pltpu.SemaphoreType.DMA((7, shards)),
            pltpu.SemaphoreType.DMA((7, shards)),
            pltpu.SemaphoreType.DMA((4, grps)),
            pltpu.SemaphoreType.DMA((4, grps)),
        ],
        compiler_params=pltpu.CompilerParams(collective_id=0, has_side_effects=True),
        name="tower_exchange",
    )(
        touched,
        block_slot.reshape(1, -1),
        slot_table.reshape(1, -1),
        emb_grads.reshape(count * block_rows, width),
        dense_x,
        dense_cot,
        w_one,
        w_two,
        w_three,
        t2,
        tf2,
        ts2,
    )
    mats = (w_one, w_two, w_three)
    outs = pl.pallas_call(
        lamb_kernel,
        out_shape=(sds(flat, F32),) * 3 + tuple(sds(w.shape, F32) for w in mats * 3),
        in_specs=[vmem] * 17,
        out_specs=(vmem,) * 12,
        name="lamb",
    )(
        emb, rate, t2, tf2, ts2, g1, g2, g3, w_one, w_two, w_three,
        first_one, first_two, first_three, second_one, second_two, second_three,
    )
    return tuple(o.reshape(table.shape) for o in outs[:3]) + tuple(outs[3:])


def solution(mesh):
    dense = (P(),) * 9
    rows = P("shard", None, None)
    return jax.shard_map(
        body,
        mesh=mesh,
        in_specs=(
            rows,
            rows,
            rows,
            P("shard"),
            P("grp", "shard"),
            P("grp", "shard", None, None),
            P(),
            P(None, ("grp", "shard")),
            P(("grp", "shard"), None),
        )
        + dense,
        out_specs=(rows,) * 3 + dense,
        check_vma=False,
    )
```

```python
import functools
import jax
import jax.numpy as jnp
from jax import lax
from jax.experimental import pallas as pl
from jax.experimental.pallas import tpu as pltpu
from jax.sharding import PartitionSpec as P

TABLES = 26
CAP = 8
HEAD = 1

beta_one = 0.9
beta_two = 0.999
corr_first = 1.0 - 0.9**10
corr_second = 1.0 - 0.999**10
adam_eps = 1e-06
decay_rate = 0.01
learn_rate = 0.1
ratio_eps = 1e-06

MESH = pl.DeviceIdType.MESH
F32 = jnp.float32
BF16 = jnp.bfloat16
NN = (((1,), (0,)), ((), ()))
NT = (((1,), (1,)), ((), ()))
TN = (((0,), (0,)), ((), ()))


def mm(a, b, dims=NN):
    return lax.dot_general(a, b, dims, preferred_element_type=F32)


def iota(shape, axis):
    return lax.broadcasted_iota(jnp.int32, shape, axis).astype(F32)


def to_col(row, eye):
    return jnp.sum(jnp.where(eye, row, 0.0), axis=1, keepdims=True)


def to_row(col, eye):
    return jnp.sum(jnp.where(eye, col, 0.0), axis=0, keepdims=True)


def square_eye(count):
    return iota((count, count), 0) == iota((count, count), 1)


def gate(pre):
    logistic = 0.5 * jnp.tanh(0.5 * pre) + 0.5
    hidden = pre * logistic
    return hidden, logistic + hidden * (1.0 - logistic)


def adam(first_in, second_in, gradient, weight):
    first_out = beta_one * first_in + (1.0 - beta_one) * gradient
    second_out = beta_two * second_in + (1.0 - beta_two) * gradient * gradient
    update = (
        first_out / corr_first / (jnp.sqrt(second_out / corr_second) + adam_eps)
        + decay_rate * weight
    )
    return first_out, second_out, update


def exchange_kernel(
    grps,
    shards,
    chunk,
    touched,
    block_slot,
    slot_table,
    emb_grads,
    w_one,
    w_three,
    w_two_in,
    x_in,
    cot_in,
    table_in,
    first_in,
    second_in,
    emb_out,
    rate_out,
    g_one,
    g_two,
    g_three,
    w1t,
    w2t,
    w2b,
    w3b,
    slope_buf,
    back_buf,
    acc_one,
    acc_two,
    acc_three,
    rows_f32,
    w_two,
    x,
    cot,
    table,
    table_first,
    table_second,
    e_send,
    e_recv,
    t_send,
    t_recv,
    t_all,
    p2_send,
    p2_recv,
    p3_send,
    p3_recv,
    z2,
    z3,
    a2,
    a3,
    s1,
    y1,
    stats,
    plane_ssem,
    plane_rsem,
    z_ssem,
    z_rsem,
    load_sem,
):
    g = lax.axis_index("grp")
    s = lax.axis_index("shard")
    width = emb_grads.shape[1]
    block_rows = 8
    count = touched.shape[1]
    slots = block_slot.shape[1]
    local_blocks = slot_table.shape[1]
    tokens = x.shape[1]
    din = x.shape[0]

    loads = [
        pltpu.make_async_copy(src, dst, load_sem.at[i])
        for i, (src, dst) in enumerate(
            (
                (w_two_in, w_two),
                (x_in, x),
                (cot_in, cot),
                (table_in, table),
                (first_in, table_first),
                (second_in, table_second),
            )
        )
    ]
    for c in loads:
        c.start()
    barrier = pltpu.get_barrier_semaphore()
    for k in range(1, shards):
        pl.semaphore_signal(barrier, inc=1, device_id=(g, lax.rem(s + k, shards)), device_id_type=MESH)
    for k in range(1, grps):
        pl.semaphore_signal(barrier, inc=1, device_id=(lax.rem(g + k, grps), s), device_id_type=MESH)

    def plane(phase, k, src, dst):
        return pltpu.make_async_remote_copy(
            src_ref=src,
            dst_ref=dst,
            send_sem=plane_ssem.at[phase, k],
            recv_sem=plane_rsem.at[phase, k],
            device_id=(g, lax.rem(s + k, shards)),
            device_id_type=MESH,
        )

    def along(phase, k, src, dst):
        return pltpu.make_async_remote_copy(
            src_ref=src,
            dst_ref=dst,
            send_sem=z_ssem.at[phase, k],
            recv_sem=z_rsem.at[phase, k],
            device_id=(lax.rem(g + k, grps), s),
            device_id_type=MESH,
        )

    def plane_scatter(phase, src, dst):
        out = [plane(phase, k, src.at[lax.rem(s + k, shards)], dst.at[s]) for k in range(1, shards)]
        for c in out:
            c.start()
        return out

    def plane_spread(phase, buf):
        out = [plane(phase, k, buf.at[s], buf.at[s]) for k in range(1, shards)]
        for c in out:
            c.start()
        return out

    def z_spread(phase, buf):
        out = [along(phase, k, buf.at[g], buf.at[g]) for k in range(1, grps)]
        for c in out:
            c.start()
        return out

    def recv(copies):
        for c in copies:
            c.wait_recv()

    eye = square_eye(count)
    touched_col = to_col(touched[...].astype(F32), eye)
    hot = touched_col == iota((count, slots), 1)
    slot_col = jnp.sum(jnp.where(hot, block_slot[...].astype(F32), 0.0), axis=1, keepdims=True)
    slot_row = to_row(slot_col, eye)
    owner_col = jnp.floor((slot_col + 0.5) / local_blocks)
    owner_row = jnp.floor((slot_row + 0.5) / local_blocks)
    local_row = slot_row - owner_row * local_blocks
    earlier = (owner_col == owner_row) & (iota((count, count), 0) < iota((count, count), 1))
    rank_row = jnp.sum(jnp.where(earlier, 1.0, 0.0), axis=0, keepdims=True)
    send_row = owner_row * CAP + rank_row
    picker = iota((shards * CAP, count), 0) == send_row
    pick_f32 = jnp.where(picker, 1.0, 0.0)
    pick_bf = pick_f32.astype(BF16)
    filled = jnp.sum(pick_f32, axis=1, keepdims=True)
    local_col = jnp.sum(jnp.where(picker, local_row, 0.0), axis=1, keepdims=True)
    local_col = jnp.where(filled > 0.5, local_col, -1.0)
    rows_f32[...] = emb_grads[...].astype(F32)
    for r in range(block_rows):
        part = rows_f32[pl.ds(r, count, stride=block_rows), :].astype(BF16)
        picked = mm(pick_bf, part).reshape(shards, CAP, width)
        e_send[:, :, r * width : (r + 1) * width] = picked.astype(BF16)
    lanes = jnp.broadcast_to(local_col, (shards * CAP, width)).reshape(shards, CAP, width)
    t_send[...] = lanes.astype(BF16)
    e_recv[g, s] = e_send[s]
    t_recv[s] = t_send[s]

    pl.semaphore_wait(barrier, shards + grps - 2)
    sends = []
    e_plane = [
        plane(0, k, e_send.at[lax.rem(s + k, shards)], e_recv.at[g, s]) for k in range(1, shards)
    ]
    for c in e_plane:
        c.start()
    t_plane = plane_scatter(1, t_send, t_recv)
    sends += e_plane + t_plane

    for c in loads[:3]:
        c.wait()
    w1t[...] = w_one[...].T.astype(BF16)
    w2t[...] = w_two[...].T.astype(BF16)
    w2b[...] = w_two[...].astype(BF16)
    w3b[...] = w_three[...].astype(BF16)
    acc_one[...] = jnp.zeros_like(acc_one)
    acc_two[...] = jnp.zeros_like(acc_two)
    acc_three[...] = jnp.zeros_like(acc_three)

    def forward(i, carry):
        tok = pl.ds(pl.multiple_of(i * chunk, chunk), chunk)
        hid, slope = gate(mm(w1t[...], x[:, tok]))
        hidden_one = hid.astype(BF16)
        slope_buf[:, tok] = slope
        hid, slope = gate(mm(w2t[...], hidden_one))
        c = cot[tok, :]
        acc_three[...] += mm(hid.astype(BF16), c)
        back = (mm(w3b[...], c, NT) * slope).astype(BF16)
        back_buf[:, tok] = back
        acc_two[...] += mm(hidden_one, back, NT)
        return carry

    def backward(i, carry):
        tok = pl.ds(pl.multiple_of(i * chunk, chunk), chunk)
        back = (mm(w2b[...], back_buf[:, tok]) * slope_buf[:, tok]).astype(BF16)
        acc_one[0:din, :] += mm(x[:, tok], back, NT)
        return carry

    steps = tokens // chunk
    head = min(HEAD, steps)
    lax.fori_loop(0, head, forward, 0)
    recv(e_plane)
    e_z = z_spread(0, e_recv)
    recv(t_plane)
    group = shards * CAP
    tag_lanes = t_all.shape[2]
    tag_eye = iota((group, tag_lanes), 0) == iota((group, tag_lanes), 1)
    tag_row = to_row(t_recv[...].astype(F32).reshape(group, width)[:, 0:1], tag_eye)
    t_all[g] = jnp.broadcast_to(tag_row, t_all.shape[1:]).astype(BF16)
    t_z = z_spread(1, t_all)
    sends += e_z + t_z
    lax.fori_loop(head, steps, forward, 0)

    p3_send[...] = acc_three[...].reshape(p3_send.shape).astype(BF16)
    p3_recv[s] = p3_send[s]
    c_p3 = plane_scatter(2, p3_send, p3_recv)
    p2_send[...] = acc_two[...].reshape(p2_send.shape).astype(BF16)
    p2_recv[s] = p2_send[s]
    parts = p2_send.shape[1]
    c_p2 = []
    for h in range(parts):
        group_p = [
            plane(6 + h, k, p2_send.at[lax.rem(s + k, shards), h], p2_recv.at[s, h])
            for k in range(1, shards)
        ]
        for c in group_p:
            c.start()
        c_p2.append(group_p)
        sends += group_p
    sends += c_p3

    lax.fori_loop(0, steps, backward, 0)
    s1[s] = acc_one[...].astype(BF16)
    c_s1 = plane_spread(3, s1)
    sends += c_s1

    def total(buf, n, *at):
        out = buf[(0,) + at].astype(F32)
        for i in range(1, n):
            out += buf[(i,) + at].astype(F32)
        return out

    def start(copies):
        for c in copies:
            c.start()
        sends.extend(copies)
        return copies

    recv(c_p3)
    z3[g] = total(p3_recv, shards).astype(BF16)
    c_z3 = z_spread(2, z3)
    c_z2 = []
    for h in range(parts):
        recv(c_p2[h])
        z2[g, h] = total(p2_recv, shards, h).astype(BF16)
        c_z2.append(start([along(4 + h, k, z2.at[g, h], z2.at[g, h]) for k in range(1, grps)]))
    recv(c_s1)
    y1[g] = total(s1, shards).astype(BF16)
    c_y1 = z_spread(3, y1)
    sends += c_z3 + c_y1

    slots_at = iota((local_blocks, group), 0)
    recv(e_z)
    recv(t_z)
    for c in loads[3:]:
        c.wait()
    matches = [
        jnp.where(slots_at == t_all[q, 0:1, 0:group].astype(F32), 1.0, 0.0) for q in range(grps)
    ]
    hits = jnp.sum(sum(matches), axis=1, keepdims=True) > 0.5
    match_t = jnp.concatenate(matches, axis=1).astype(BF16)
    row_weight = jnp.zeros((local_blocks, width), F32)
    row_update = jnp.zeros((local_blocks, width), F32)
    for r in range(block_rows):
        at = pl.ds(r, local_blocks, stride=block_rows)
        rows = e_recv[:, :, :, r * width : (r + 1) * width].astype(F32)
        summed = mm(match_t, rows.reshape(grps * group, width).astype(BF16))
        emb_out[at, :] = summed
        weight = table[at, :]
        update = adam(table_first[at, :], table_second[at, :], summed, weight)[2]
        update = jnp.where(hits, update, 0.0)
        row_weight += weight * weight
        row_update += update * update
    slot_eye = square_eye(local_blocks)
    table_col = to_col(slot_table[...].astype(F32), slot_eye)
    table_hot = table_col == iota((local_blocks, 128), 1)
    weight_col = jnp.sum(row_weight, axis=1, keepdims=True)
    update_col = jnp.sum(row_update, axis=1, keepdims=True)
    stats[s] = jnp.concatenate(
        [
            jnp.sum(jnp.where(table_hot, weight_col, 0.0), axis=0, keepdims=True),
            jnp.sum(jnp.where(table_hot, update_col, 0.0), axis=0, keepdims=True),
            jnp.zeros((6, 128), F32),
        ],
        axis=0,
    )
    c_st = plane_spread(4, stats)
    sends += c_st

    recv(c_z3)
    a3[s] = total(z3, grps).astype(BF16)
    c_a3 = plane_spread(5, a3)
    sends += c_a3
    c_a2 = []
    for h in range(parts):
        recv(c_z2[h])
        a2[s, h] = total(z2, grps, h).astype(BF16)
        c_a2 += start(
            [plane(6 + parts + h, k, a2.at[s, h], a2.at[s, h]) for k in range(1, shards)]
        )
    recv(c_st)
    tot = total(stats, shards)
    ratio = jnp.sqrt(tot[0:1]) / (jnp.sqrt(tot[1:2]) + ratio_eps)
    ratio_col = jnp.sum(jnp.where(table_hot, ratio, 0.0), axis=1, keepdims=True)
    rate = jnp.where(hits, learn_rate * ratio_col, -1.0)
    rate = jnp.broadcast_to(rate, (local_blocks, width))
    for r in range(block_rows):
        rate_out[pl.ds(r, local_blocks, stride=block_rows), :] = rate
    recv(c_y1)
    g_one[...] = total(y1, grps)
    recv(c_a2)
    g_two[...] = a2[...].astype(F32).reshape(g_two.shape)
    recv(c_a3)
    g_three[...] = a3[...].astype(F32).reshape(g_three.shape)
    for c in sends:
        c.wait_send()


def lamb_kernel(*refs):
    ins, outs = refs[:17], refs[17:29]
    bufs, stage = refs[29:46], refs[46:58]
    in_sem, out_sem = refs[58:]
    loads = [pltpu.make_async_copy(a, b, in_sem.at[i]) for i, (a, b) in enumerate(zip(ins, bufs))]
    stores = [
        pltpu.make_async_copy(a, b, out_sem.at[i]) for i, (a, b) in enumerate(zip(stage, outs))
    ]
    dense = [(5 + j, 8 + j, 11 + j, 14 + j) for j in (1, 0, 2)]
    for group in dense + [range(5)]:
        for i in group:
            loads[i].start()
    for j, group in zip((1, 0, 2), dense):
        for i in group:
            loads[i].wait()
        grad, w, f, q = (bufs[i] for i in group)
        weight = w[...]
        first, second, update = adam(f[...], q[...], grad[0 : w.shape[0], :].astype(F32), weight)
        stage[6 + j][...] = first
        stage[9 + j][...] = second
        stores[6 + j].start()
        stores[9 + j].start()
        trust = jnp.sqrt(jnp.sum(weight * weight, keepdims=True)) / (
            jnp.sqrt(jnp.sum(update * update, keepdims=True)) + ratio_eps
        )
        stage[3 + j][...] = weight - learn_rate * trust * update
        stores[3 + j].start()
    for i in range(5):
        loads[i].wait()
    emb, rate, table, tf, ts = bufs[:5]
    mask = rate[...] >= 0.0
    first, second, update = adam(tf[...], ts[...], emb[...], table[...])
    stage[1][...] = jnp.where(mask, first, tf[...])
    stores[1].start()
    stage[2][...] = jnp.where(mask, second, ts[...])
    stores[2].start()
    stage[0][...] = jnp.where(mask, table[...] - rate[...] * update, table[...])
    stores[0].start()
    for c in stores:
        c.wait()


def body(
    table, table_first, table_second, slot_table, touched, emb_grads, block_slot,
    dense_x, dense_cot, w_one, w_two, w_three, first_one, first_two, first_three,
    second_one, second_two, second_three,
):
    shards = lax.axis_size("shard")
    grps = lax.axis_size("grp")
    blocks, block_rows, width = table.shape
    count = touched.shape[1]
    din, tokens = dense_x.shape
    h_one, h_two = w_two.shape
    out_dim = w_three.shape[1]
    chunk = min(1024, tokens)
    din_pad = -(-din // 16) * 16
    flat = (blocks * block_rows, width)
    e_width = block_rows * width
    tag_width = max(128, shards * CAP)
    r2 = h_one // shards
    r3 = h_two // shards
    parts = min(4, max(1, r2 // 16))
    anywhere = pl.BlockSpec(memory_space=pl.ANY)
    vmem = pl.BlockSpec(memory_space=pltpu.VMEM)
    t2, tf2, ts2 = (a.reshape(flat) for a in (table, table_first, table_second))
    sds = jax.ShapeDtypeStruct
    emb, rate, g1, g2, g3 = pl.pallas_call(
        functools.partial(exchange_kernel, grps, shards, chunk),
        out_shape=(
            sds(flat, F32),
            sds(flat, F32),
            sds((din_pad, h_one), F32),
            sds((h_one, h_two), F32),
            sds((h_two, out_dim), F32),
        ),
        in_specs=[vmem] * 6 + [anywhere] * 6,
        out_specs=(vmem,) * 5,
        scratch_shapes=[
            pltpu.VMEM((h_one, din), BF16),
            pltpu.VMEM((h_two, h_one), BF16),
            pltpu.VMEM((h_one, h_two), BF16),
            pltpu.VMEM((h_two, out_dim), BF16),
            pltpu.VMEM((h_one, tokens), F32),
            pltpu.VMEM((h_two, tokens), BF16),
            pltpu.VMEM((din_pad, h_one), F32),
            pltpu.VMEM((h_one, h_two), F32),
            pltpu.VMEM((h_two, out_dim), F32),
            pltpu.VMEM((count * block_rows, width), F32),
            pltpu.VMEM(w_two.shape, F32),
            pltpu.VMEM(dense_x.shape, BF16),
            pltpu.VMEM(dense_cot.shape, BF16),
            pltpu.VMEM(flat, F32),
            pltpu.VMEM(flat, F32),
            pltpu.VMEM(flat, F32),
            pltpu.VMEM((shards, CAP, e_width), BF16),
            pltpu.VMEM((grps, shards, CAP, e_width), BF16),
            pltpu.VMEM((shards, CAP, width), BF16),
            pltpu.VMEM((shards, CAP, width), BF16),
            pltpu.VMEM((grps, 16, tag_width), BF16),
            pltpu.VMEM((shards, parts, r2 // parts, h_two), BF16),
            pltpu.VMEM((shards, parts, r2 // parts, h_two), BF16),
            pltpu.VMEM((shards, r3, out_dim), BF16),
            pltpu.VMEM((shards, r3, out_dim), BF16),
            pltpu.VMEM((grps, parts, r2 // parts, h_two), BF16),
            pltpu.VMEM((grps, r3, out_dim), BF16),
            pltpu.VMEM((shards, parts, r2 // parts, h_two), BF16),
            pltpu.VMEM((shards, r3, out_dim), BF16),
            pltpu.VMEM((shards, din_pad, h_one), BF16),
            pltpu.VMEM((grps, din_pad, h_one), BF16),
            pltpu.VMEM((shards, 8, 128), F32),
            pltpu.SemaphoreType.DMA((6 + 2 * parts, shards)),
            pltpu.SemaphoreType.DMA((6 + 2 * parts, shards)),
            pltpu.SemaphoreType.DMA((4 + parts, grps)),
            pltpu.SemaphoreType.DMA((4 + parts, grps)),
            pltpu.SemaphoreType.DMA((6,)),
        ],
        compiler_params=pltpu.CompilerParams(collective_id=0, has_side_effects=True),
        name="tower_exchange",
    )(
        touched,
        block_slot.reshape(1, -1),
        slot_table.reshape(1, -1),
        emb_grads.reshape(count * block_rows, width),
        w_one,
        w_three,
        w_two,
        dense_x,
        dense_cot,
        t2,
        tf2,
        ts2,
    )
    mats = (w_one, w_two, w_three)
    args = (
        emb, rate, t2, tf2, ts2, g1, g2, g3, w_one, w_two, w_three,
        first_one, first_two, first_three, second_one, second_two, second_three,
    )
    shapes = (sds(flat, F32),) * 3 + tuple(sds(w.shape, F32) for w in mats * 3)
    outs = pl.pallas_call(
        lamb_kernel,
        out_shape=shapes,
        in_specs=[anywhere] * 17,
        out_specs=(anywhere,) * 12,
        scratch_shapes=[pltpu.VMEM(a.shape, a.dtype) for a in args + shapes]
        + [pltpu.SemaphoreType.DMA((17,)), pltpu.SemaphoreType.DMA((12,))],
        name="lamb",
    )(*args)
    return tuple(o.reshape(table.shape) for o in outs[:3]) + tuple(outs[3:])


def solution(mesh):
    dense = (P(),) * 9
    rows = P("shard", None, None)
    return jax.shard_map(
        body,
        mesh=mesh,
        in_specs=(
            rows,
            rows,
            rows,
            P("shard"),
            P("grp", "shard"),
            P("grp", "shard", None, None),
            P(),
            P(None, ("grp", "shard")),
            P(("grp", "shard"), None),
        )
        + dense,
        out_specs=(rows,) * 3 + dense,
        check_vma=False,
    )
```

```python
import functools
import jax
import jax.numpy as jnp
from jax import lax
from jax.experimental import pallas as pl
from jax.experimental.pallas import tpu as pltpu
from jax.sharding import PartitionSpec as P

TABLES = 26
CAP = 8
HEAD = 0

beta_one = 0.9
beta_two = 0.999
corr_first = 1.0 - 0.9**10
corr_second = 1.0 - 0.999**10
adam_eps = 1e-06
decay_rate = 0.01
learn_rate = 0.1
ratio_eps = 1e-06

MESH = pl.DeviceIdType.MESH
F32 = jnp.float32
BF16 = jnp.bfloat16
NN = (((1,), (0,)), ((), ()))
NT = (((1,), (1,)), ((), ()))
TN = (((0,), (0,)), ((), ()))


def mm(a, b, dims=NN):
    return lax.dot_general(a, b, dims, preferred_element_type=F32)


def iota(shape, axis):
    return lax.broadcasted_iota(jnp.int32, shape, axis).astype(F32)


def to_col(row, eye):
    return jnp.sum(jnp.where(eye, row, 0.0), axis=1, keepdims=True)


def to_row(col, eye):
    return jnp.sum(jnp.where(eye, col, 0.0), axis=0, keepdims=True)


def square_eye(count):
    return iota((count, count), 0) == iota((count, count), 1)


def gate(pre):
    logistic = 0.5 * jnp.tanh(0.5 * pre) + 0.5
    hidden = pre * logistic
    return hidden, logistic + hidden * (1.0 - logistic)


def adam(first_in, second_in, gradient, weight):
    first_out = beta_one * first_in + (1.0 - beta_one) * gradient
    second_out = beta_two * second_in + (1.0 - beta_two) * gradient * gradient
    update = (
        first_out / corr_first / (jnp.sqrt(second_out / corr_second) + adam_eps)
        + decay_rate * weight
    )
    return first_out, second_out, update


def exchange_kernel(
    grps,
    shards,
    chunk,
    touched,
    block_slot,
    slot_table,
    emb_grads,
    w_one,
    w_three,
    w_two_in,
    x_in,
    cot_in,
    table_in,
    first_in,
    second_in,
    emb_out,
    rate_out,
    g_one,
    g_two,
    g_three,
    w1t,
    w2t,
    w2b,
    w3b,
    slope_buf,
    back_buf,
    acc_one,
    acc_two,
    acc_three,
    rows_f32,
    w_two,
    x,
    cot,
    table,
    table_first,
    table_second,
    e_send,
    e_recv,
    t_send,
    t_recv,
    t_all,
    p2_send,
    p2_recv,
    p3_send,
    p3_recv,
    z2,
    z3,
    a2,
    a3,
    s1,
    y1,
    stats,
    plane_ssem,
    plane_rsem,
    z_ssem,
    z_rsem,
    load_sem,
):
    g = lax.axis_index("grp")
    s = lax.axis_index("shard")
    width = emb_grads.shape[1]
    block_rows = 8
    count = touched.shape[1]
    slots = block_slot.shape[1]
    local_blocks = slot_table.shape[1]
    tokens = x.shape[1]
    din = x.shape[0]

    loads = [
        pltpu.make_async_copy(src, dst, load_sem.at[i])
        for i, (src, dst) in enumerate(
            (
                (w_two_in, w_two),
                (x_in, x),
                (cot_in, cot),
                (table_in, table),
                (first_in, table_first),
                (second_in, table_second),
            )
        )
    ]
    for c in loads:
        c.start()
    barrier = pltpu.get_barrier_semaphore()
    for k in range(1, shards):
        pl.semaphore_signal(barrier, inc=1, device_id=(g, lax.rem(s + k, shards)), device_id_type=MESH)
    for k in range(1, grps):
        pl.semaphore_signal(barrier, inc=1, device_id=(lax.rem(g + k, grps), s), device_id_type=MESH)

    def plane(phase, k, src, dst):
        return pltpu.make_async_remote_copy(
            src_ref=src,
            dst_ref=dst,
            send_sem=plane_ssem.at[phase, k],
            recv_sem=plane_rsem.at[phase, k],
            device_id=(g, lax.rem(s + k, shards)),
            device_id_type=MESH,
        )

    def along(phase, k, src, dst):
        return pltpu.make_async_remote_copy(
            src_ref=src,
            dst_ref=dst,
            send_sem=z_ssem.at[phase, k],
            recv_sem=z_rsem.at[phase, k],
            device_id=(lax.rem(g + k, grps), s),
            device_id_type=MESH,
        )

    def plane_scatter(phase, src, dst):
        out = [plane(phase, k, src.at[lax.rem(s + k, shards)], dst.at[s]) for k in range(1, shards)]
        for c in out:
            c.start()
        return out

    def plane_spread(phase, buf):
        out = [plane(phase, k, buf.at[s], buf.at[s]) for k in range(1, shards)]
        for c in out:
            c.start()
        return out

    def z_spread(phase, buf):
        out = [along(phase, k, buf.at[g], buf.at[g]) for k in range(1, grps)]
        for c in out:
            c.start()
        return out

    def recv(copies):
        for c in copies:
            c.wait_recv()

    eye = square_eye(count)
    touched_col = to_col(touched[...].astype(F32), eye)
    hot = touched_col == iota((count, slots), 1)
    slot_col = jnp.sum(jnp.where(hot, block_slot[...].astype(F32), 0.0), axis=1, keepdims=True)
    slot_row = to_row(slot_col, eye)
    owner_col = jnp.floor((slot_col + 0.5) / local_blocks)
    owner_row = jnp.floor((slot_row + 0.5) / local_blocks)
    local_row = slot_row - owner_row * local_blocks
    earlier = (owner_col == owner_row) & (iota((count, count), 0) < iota((count, count), 1))
    rank_row = jnp.sum(jnp.where(earlier, 1.0, 0.0), axis=0, keepdims=True)
    send_row = owner_row * CAP + rank_row
    picker = iota((shards * CAP, count), 0) == send_row
    pick_f32 = jnp.where(picker, 1.0, 0.0)
    pick_bf = pick_f32.astype(BF16)
    filled = jnp.sum(pick_f32, axis=1, keepdims=True)
    local_col = jnp.sum(jnp.where(picker, local_row, 0.0), axis=1, keepdims=True)
    local_col = jnp.where(filled > 0.5, local_col, -1.0)
    rows_f32[...] = emb_grads[...].astype(F32)
    for r in range(block_rows):
        part = rows_f32[pl.ds(r, count, stride=block_rows), :].astype(BF16)
        picked = mm(pick_bf, part).reshape(shards, CAP, width)
        e_send[:, :, r * width : (r + 1) * width] = picked.astype(BF16)
    lanes = jnp.broadcast_to(local_col, (shards * CAP, width)).reshape(shards, CAP, width)
    t_send[...] = lanes.astype(BF16)
    e_recv[g, s] = e_send[s]
    t_recv[s] = t_send[s]

    pl.semaphore_wait(barrier, shards + grps - 2)
    sends = []
    e_plane = [
        plane(0, k, e_send.at[lax.rem(s + k, shards)], e_recv.at[g, s]) for k in range(1, shards)
    ]
    for c in e_plane:
        c.start()
    t_plane = plane_scatter(1, t_send, t_recv)
    sends += e_plane + t_plane

    for c in loads[:3]:
        c.wait()
    w1t[...] = w_one[...].T.astype(BF16)
    w2t[...] = w_two[...].T.astype(BF16)
    w2b[...] = w_two[...].astype(BF16)
    w3b[...] = w_three[...].astype(BF16)
    acc_one[...] = jnp.zeros_like(acc_one)
    acc_two[...] = jnp.zeros_like(acc_two)
    acc_three[...] = jnp.zeros_like(acc_three)

    def forward(i, carry):
        tok = pl.ds(pl.multiple_of(i * chunk, chunk), chunk)
        hid, slope = gate(mm(w1t[...], x[:, tok]))
        hidden_one = hid.astype(BF16)
        slope_buf[:, tok] = slope
        hid, slope = gate(mm(w2t[...], hidden_one))
        c = cot[tok, :]
        acc_three[...] += mm(hid.astype(BF16), c)
        back = (mm(w3b[...], c, NT) * slope).astype(BF16)
        back_buf[:, tok] = back
        acc_two[...] += mm(hidden_one, back, NT)
        return carry

    def backward(i, carry):
        tok = pl.ds(pl.multiple_of(i * chunk, chunk), chunk)
        back = (mm(w2b[...], back_buf[:, tok]) * slope_buf[:, tok]).astype(BF16)
        acc_one[0:din, :] += mm(x[:, tok], back, NT)
        return carry

    steps = tokens // chunk
    head = min(HEAD, steps)
    if head:
        lax.fori_loop(0, head, forward, 0)
    recv(e_plane)
    e_z = z_spread(0, e_recv)
    recv(t_plane)
    group = shards * CAP
    tag_lanes = t_all.shape[2]
    tag_eye = iota((group, tag_lanes), 0) == iota((group, tag_lanes), 1)
    tag_row = to_row(t_recv[...].astype(F32).reshape(group, width)[:, 0:1], tag_eye)
    t_all[g] = jnp.broadcast_to(tag_row, t_all.shape[1:]).astype(BF16)
    t_z = z_spread(1, t_all)
    sends += e_z + t_z
    lax.fori_loop(head, steps, forward, 0)

    p3_send[...] = acc_three[...].reshape(p3_send.shape).astype(BF16)
    p3_recv[s] = p3_send[s]
    c_p3 = plane_scatter(2, p3_send, p3_recv)
    p2_send[...] = acc_two[...].reshape(p2_send.shape).astype(BF16)
    p2_recv[s] = p2_send[s]
    parts = p2_send.shape[1]
    c_p2 = []
    for h in range(parts):
        group_p = [
            plane(6 + h, k, p2_send.at[lax.rem(s + k, shards), h], p2_recv.at[s, h])
            for k in range(1, shards)
        ]
        for c in group_p:
            c.start()
        c_p2.append(group_p)
        sends += group_p
    sends += c_p3

    lax.fori_loop(0, steps, backward, 0)
    s1[s] = acc_one[...].astype(BF16)
    c_s1 = plane_spread(3, s1)
    sends += c_s1

    def total(buf, n, *at):
        out = buf[(0,) + at].astype(F32)
        for i in range(1, n):
            out += buf[(i,) + at].astype(F32)
        return out

    def start(copies):
        for c in copies:
            c.start()
        sends.extend(copies)
        return copies

    recv(c_p3)
    z3[g] = total(p3_recv, shards).astype(BF16)
    c_z3 = z_spread(2, z3)
    c_z2 = []
    for h in range(parts):
        recv(c_p2[h])
        z2[g, h] = total(p2_recv, shards, h).astype(BF16)
        c_z2.append(start([along(4 + h, k, z2.at[g, h], z2.at[g, h]) for k in range(1, grps)]))
    recv(c_s1)
    y1[g] = total(s1, shards).astype(BF16)
    c_y1 = z_spread(3, y1)
    sends += c_z3 + c_y1

    slots_at = iota((local_blocks, group), 0)
    recv(e_z)
    recv(t_z)
    for c in loads[3:]:
        c.wait()
    matches = [
        jnp.where(slots_at == t_all[q, 0:1, 0:group].astype(F32), 1.0, 0.0) for q in range(grps)
    ]
    hits = jnp.sum(sum(matches), axis=1, keepdims=True) > 0.5
    match_t = jnp.concatenate(matches, axis=1).astype(BF16)
    row_weight = jnp.zeros((local_blocks, width), F32)
    row_update = jnp.zeros((local_blocks, width), F32)
    for r in range(block_rows):
        at = pl.ds(r, local_blocks, stride=block_rows)
        rows = e_recv[:, :, :, r * width : (r + 1) * width].astype(F32)
        summed = mm(match_t, rows.reshape(grps * group, width).astype(BF16))
        emb_out[at, :] = summed
        weight = table[at, :]
        update = adam(table_first[at, :], table_second[at, :], summed, weight)[2]
        update = jnp.where(hits, update, 0.0)
        row_weight += weight * weight
        row_update += update * update
    slot_eye = square_eye(local_blocks)
    table_col = to_col(slot_table[...].astype(F32), slot_eye)
    table_hot = table_col == iota((local_blocks, 128), 1)
    weight_col = jnp.sum(row_weight, axis=1, keepdims=True)
    update_col = jnp.sum(row_update, axis=1, keepdims=True)
    stats[s] = jnp.concatenate(
        [
            jnp.sum(jnp.where(table_hot, weight_col, 0.0), axis=0, keepdims=True),
            jnp.sum(jnp.where(table_hot, update_col, 0.0), axis=0, keepdims=True),
            jnp.zeros((6, 128), F32),
        ],
        axis=0,
    )
    c_st = plane_spread(4, stats)
    sends += c_st

    recv(c_z3)
    a3[s] = total(z3, grps).astype(BF16)
    c_a3 = plane_spread(5, a3)
    sends += c_a3
    c_a2 = []
    for h in range(parts):
        recv(c_z2[h])
        a2[s, h] = total(z2, grps, h).astype(BF16)
        c_a2 += start(
            [plane(6 + parts + h, k, a2.at[s, h], a2.at[s, h]) for k in range(1, shards)]
        )
    recv(c_st)
    tot = total(stats, shards)
    ratio = jnp.sqrt(tot[0:1]) / (jnp.sqrt(tot[1:2]) + ratio_eps)
    ratio_col = jnp.sum(jnp.where(table_hot, ratio, 0.0), axis=1, keepdims=True)
    rate = jnp.where(hits, learn_rate * ratio_col, -1.0)
    rate = jnp.broadcast_to(rate, (local_blocks, width))
    for r in range(block_rows):
        rate_out[pl.ds(r, local_blocks, stride=block_rows), :] = rate
    recv(c_y1)
    g_one[...] = total(y1, grps)
    recv(c_a2)
    g_two[...] = a2[...].astype(F32).reshape(g_two.shape)
    recv(c_a3)
    g_three[...] = a3[...].astype(F32).reshape(g_three.shape)
    for c in sends:
        c.wait_send()


def lamb_kernel(*refs):
    ins, outs = refs[:17], refs[17:29]
    bufs, stage = refs[29:46], refs[46:58]
    in_sem, out_sem = refs[58:]
    loads = [pltpu.make_async_copy(a, b, in_sem.at[i]) for i, (a, b) in enumerate(zip(ins, bufs))]
    stores = [
        pltpu.make_async_copy(a, b, out_sem.at[i]) for i, (a, b) in enumerate(zip(stage, outs))
    ]
    dense = [(5 + j, 8 + j, 11 + j, 14 + j) for j in (1, 0, 2)]
    for group in dense + [range(5)]:
        for i in group:
            loads[i].start()
    for j, group in zip((1, 0, 2), dense):
        for i in group:
            loads[i].wait()
        grad, w, f, q = (bufs[i] for i in group)
        weight = w[...]
        first, second, update = adam(f[...], q[...], grad[0 : w.shape[0], :].astype(F32), weight)
        stage[6 + j][...] = first
        stage[9 + j][...] = second
        stores[6 + j].start()
        stores[9 + j].start()
        trust = jnp.sqrt(jnp.sum(weight * weight, keepdims=True)) / (
            jnp.sqrt(jnp.sum(update * update, keepdims=True)) + ratio_eps
        )
        stage[3 + j][...] = weight - learn_rate * trust * update
        stores[3 + j].start()
    for i in range(5):
        loads[i].wait()
    emb, rate, table, tf, ts = bufs[:5]
    mask = rate[...] >= 0.0
    first, second, update = adam(tf[...], ts[...], emb[...], table[...])
    stage[1][...] = jnp.where(mask, first, tf[...])
    stores[1].start()
    stage[2][...] = jnp.where(mask, second, ts[...])
    stores[2].start()
    stage[0][...] = jnp.where(mask, table[...] - rate[...] * update, table[...])
    stores[0].start()
    for c in stores:
        c.wait()


def body(
    table, table_first, table_second, slot_table, touched, emb_grads, block_slot,
    dense_x, dense_cot, w_one, w_two, w_three, first_one, first_two, first_three,
    second_one, second_two, second_three,
):
    shards = lax.axis_size("shard")
    grps = lax.axis_size("grp")
    blocks, block_rows, width = table.shape
    count = touched.shape[1]
    din, tokens = dense_x.shape
    h_one, h_two = w_two.shape
    out_dim = w_three.shape[1]
    chunk = min(1024, tokens)
    din_pad = -(-din // 16) * 16
    flat = (blocks * block_rows, width)
    e_width = block_rows * width
    tag_width = max(128, shards * CAP)
    r2 = h_one // shards
    r3 = h_two // shards
    parts = min(4, max(1, r2 // 16))
    anywhere = pl.BlockSpec(memory_space=pl.ANY)
    vmem = pl.BlockSpec(memory_space=pltpu.VMEM)
    t2, tf2, ts2 = (a.reshape(flat) for a in (table, table_first, table_second))
    sds = jax.ShapeDtypeStruct
    emb, rate, g1, g2, g3 = pl.pallas_call(
        functools.partial(exchange_kernel, grps, shards, chunk),
        out_shape=(
            sds(flat, F32),
            sds(flat, F32),
            sds((din_pad, h_one), F32),
            sds((h_one, h_two), F32),
            sds((h_two, out_dim), F32),
        ),
        in_specs=[vmem] * 6 + [anywhere] * 6,
        out_specs=(vmem,) * 5,
        scratch_shapes=[
            pltpu.VMEM((h_one, din), BF16),
            pltpu.VMEM((h_two, h_one), BF16),
            pltpu.VMEM((h_one, h_two), BF16),
            pltpu.VMEM((h_two, out_dim), BF16),
            pltpu.VMEM((h_one, tokens), F32),
            pltpu.VMEM((h_two, tokens), BF16),
            pltpu.VMEM((din_pad, h_one), F32),
            pltpu.VMEM((h_one, h_two), F32),
            pltpu.VMEM((h_two, out_dim), F32),
            pltpu.VMEM((count * block_rows, width), F32),
            pltpu.VMEM(w_two.shape, F32),
            pltpu.VMEM(dense_x.shape, BF16),
            pltpu.VMEM(dense_cot.shape, BF16),
            pltpu.VMEM(flat, F32),
            pltpu.VMEM(flat, F32),
            pltpu.VMEM(flat, F32),
            pltpu.VMEM((shards, CAP, e_width), BF16),
            pltpu.VMEM((grps, shards, CAP, e_width), BF16),
            pltpu.VMEM((shards, CAP, width), BF16),
            pltpu.VMEM((shards, CAP, width), BF16),
            pltpu.VMEM((grps, 16, tag_width), BF16),
            pltpu.VMEM((shards, parts, r2 // parts, h_two), BF16),
            pltpu.VMEM((shards, parts, r2 // parts, h_two), BF16),
            pltpu.VMEM((shards, r3, out_dim), BF16),
            pltpu.VMEM((shards, r3, out_dim), BF16),
            pltpu.VMEM((grps, parts, r2 // parts, h_two), BF16),
            pltpu.VMEM((grps, r3, out_dim), BF16),
            pltpu.VMEM((shards, parts, r2 // parts, h_two), BF16),
            pltpu.VMEM((shards, r3, out_dim), BF16),
            pltpu.VMEM((shards, din_pad, h_one), BF16),
            pltpu.VMEM((grps, din_pad, h_one), BF16),
            pltpu.VMEM((shards, 8, 128), F32),
            pltpu.SemaphoreType.DMA((6 + 2 * parts, shards)),
            pltpu.SemaphoreType.DMA((6 + 2 * parts, shards)),
            pltpu.SemaphoreType.DMA((4 + parts, grps)),
            pltpu.SemaphoreType.DMA((4 + parts, grps)),
            pltpu.SemaphoreType.DMA((6,)),
        ],
        compiler_params=pltpu.CompilerParams(collective_id=0, has_side_effects=True),
        name="tower_exchange",
    )(
        touched,
        block_slot.reshape(1, -1),
        slot_table.reshape(1, -1),
        emb_grads.reshape(count * block_rows, width),
        w_one,
        w_three,
        w_two,
        dense_x,
        dense_cot,
        t2,
        tf2,
        ts2,
    )
    mats = (w_one, w_two, w_three)
    args = (
        emb, rate, t2, tf2, ts2, g1, g2, g3, w_one, w_two, w_three,
        first_one, first_two, first_three, second_one, second_two, second_three,
    )
    shapes = (sds(flat, F32),) * 3 + tuple(sds(w.shape, F32) for w in mats * 3)
    outs = pl.pallas_call(
        lamb_kernel,
        out_shape=shapes,
        in_specs=[anywhere] * 17,
        out_specs=(anywhere,) * 12,
        scratch_shapes=[pltpu.VMEM(a.shape, a.dtype) for a in args + shapes]
        + [pltpu.SemaphoreType.DMA((17,)), pltpu.SemaphoreType.DMA((12,))],
        name="lamb",
    )(*args)
    return tuple(o.reshape(table.shape) for o in outs[:3]) + tuple(outs[3:])


def solution(mesh):
    dense = (P(),) * 9
    rows = P("shard", None, None)
    return jax.shard_map(
        body,
        mesh=mesh,
        in_specs=(
            rows,
            rows,
            rows,
            P("shard"),
            P("grp", "shard"),
            P("grp", "shard", None, None),
            P(),
            P(None, ("grp", "shard")),
            P(("grp", "shard"), None),
        )
        + dense,
        out_specs=(rows,) * 3 + dense,
        check_vma=False,
    )
```
